32 devices in a mesh: dp: 4 (over x, core), mp: 8 (over z, y).
Axes of the slice: x: 2, y: 2, z: 4, core: 2. Of those that a mesh axis runs over, the one named last changes fastest.
Arguments:
- tokens: bfloat16 [16384, 1792], P(('dp', 'mp')), may hold values from -12 to 12
- first_norm_gain: float32 [1792], replicated, may hold values from 0.25 to 1.75
- query_weight: bfloat16 [1792, 896], replicated, may hold values from -0.144098955 to 0.144098955
- key_weight: bfloat16 [1792, 896], replicated, may hold values from -3.5670397 to 3.5670397
- value_weight: bfloat16 [1792, 896], replicated, may hold values from -0.125 to 0.125
- output_weight: bfloat16 [896, 1792], replicated, may hold values from -0.1875 to 0.1875
- lengths: int32 [256], P(('dp', 'mp')), may hold values from 1 to 64, as said below
- request_adapter: int32 [256], P(('dp', 'mp')), may hold values from 0 to 31, as said below
- slot_adapter_ids: int32 [32], replicated, may hold values from 0 to 31, as said below
- plugin_shrink_maps: bfloat16 [32, 1792, 32], P('mp'), may hold values from -0.125 to 0.125
- plugin_grow_maps: bfloat16 [32, 2, 16, 896], P('mp'), may hold values from -1.5 to 1.5
- device_token_order: int32 [32, 512], P(('dp', 'mp')), may hold values from 0 to 511, each once within a row
- second_norm_gain: float32 [1792], replicated, may hold values from 0.25 to 1.75
- gate_weight: bfloat16 [1792, 3584], P(('dp', 'mp')), may hold values from -0.125 to 0.125
- up_weight: bfloat16 [1792, 3584], P(('dp', 'mp')), may hold values from -0.125 to 0.125
Outputs:
- residual: bfloat16 [16384, 1792], P(('dp', 'mp'))
- hidden: bfloat16 [16384, 3584], P(('dp', 'mp'))
The draws below stay inside these ranges and needn't reach their ends.
Inputs may be any that keep to these rules, and one draw needn't show every extreme that they name: `slot_adapter_ids`: a permutation of the adapter ids; slot s lives on index s // 4 of mp. `request_adapter`: the 8 requests of one device use adapters whose slots lie on distinct indices of mp. `lengths`: on every device some request has length 64.
All inputs are finite; a program needn't handle non-finite values.
Results may differ from the reference program's by a relative error of at most 0.011.
Values may be sent and summed in bfloat16 or wider, within the bound.
A program may use at most 192 MiB of HBM per device.

```python
import jax
import jax.numpy as jnp
from jax import lax

EMBED_SPAN = 1792
HEADS = 8
HD = 112
FF = 3584
LATENT_BREADTH = 16
APD = 4
REQ_DEV = 8
SLOTR = 64
WINDOW = 32
SINKS = 4
ATTN_CHANNELS = 896
TOK_DEV = 512
REQUESTS = 256
TOKENS = 16384
TOTAL_PLUGINS = 32
N_MP = 8
DEVICES = 32


def shared_table(key):
    return jax.random.permutation(jax.random.fold_in(key, 11), TOTAL_PLUGINS).astype(jnp.int32)


def draw_slot_adapter_ids(key, part):
    return shared_table(key)


def draw_request_adapter(key, part):
    table = shared_table(key)
    device_count = REQUESTS // REQ_DEV
    scores = jax.random.randint(jax.random.fold_in(key, 12), (device_count, N_MP), 0, 1 << 20) * N_MP
    scores = scores + jnp.arange(N_MP, dtype=jnp.int32)[None, :]
    owners = jnp.argsort(scores, axis=1, stable=True)[:, :REQ_DEV].astype(jnp.int32)
    within = jax.random.randint(jax.random.fold_in(key, 13), (device_count, REQ_DEV), 0, APD)
    slot_ids = owners * APD + within
    return table[slot_ids].reshape(REQUESTS).astype(jnp.int32)


def draw_lengths(key, part):
    device_count = REQUESTS // REQ_DEV
    drawn = jax.random.randint(jax.random.fold_in(key, 21), (device_count, REQ_DEV), 1, SLOTR + 1)
    chosen = jax.random.randint(jax.random.fold_in(key, 22), (device_count, 1), 0, REQ_DEV)
    filled = jnp.where(jnp.arange(REQ_DEV)[None, :] == chosen, SLOTR, drawn)
    return filled.reshape(REQUESTS).astype(jnp.int32)


def draw_tokens(key, part):
    rest = jnp.clip(jax.random.normal(jax.random.fold_in(key, 31), (TOKENS, EMBED_SPAN), jnp.float32), -6.0, 6.0)
    return rest.astype(jnp.bfloat16)


def query_table(key):
    drawn = jax.random.normal(jax.random.fold_in(key, 41), (EMBED_SPAN, ATTN_CHANNELS), jnp.float32)
    return jnp.clip(drawn, -6.0, 6.0) * EMBED_SPAN ** (-0.5)


def draw_query_weight(key, part):
    return query_table(key).astype(jnp.bfloat16)


def draw_key_weight(key, part):
    drawn = jax.random.normal(jax.random.fold_in(key, 42), (EMBED_SPAN, ATTN_CHANNELS), jnp.float32)
    own = jnp.clip(drawn, -6.0, 6.0) * EMBED_SPAN ** (-0.5)
    return own.astype(jnp.bfloat16)


def steps_of(key, extent, shards, smallest, high):
    factor_of, own = 1.0, jax.random.fold_in(key, 6)
    for dim, blocks in shards:
        heights = jnp.exp(jax.random.uniform(jax.random.fold_in(own, dim), (blocks,), jnp.float32, smallest / len(shards), high / len(shards)))
        factor_of = factor_of * jnp.repeat(heights, extent[dim] // blocks).reshape([-1 if axis == dim else 1 for axis in range(len(extent))])
    return factor_of


def scatter_about(own_key, dims, scale, reach, split=(), kind=jnp.bfloat16):
    values = scale * jax.random.normal(own_key, dims, jnp.float32)
    if split:
        values = values * steps_of(own_key, dims, split, -0.22, 0.18)
    return jnp.clip(values, -reach, reach).astype(kind)


def setup_inputs(seed: int = 0) -> dict:
    keys = jax.random.split(jax.random.key(seed), 16)
    return {
        "tokens": draw_tokens(jax.random.fold_in(keys[15], 71), 0),
        "first_norm_gain": jnp.clip(1.0 + 0.15 * jax.random.normal(keys[1], (EMBED_SPAN,), jnp.float32), 0.25, 1.75),
        "query_weight": draw_query_weight(jax.random.fold_in(keys[15], 71), 0),
        "key_weight": draw_key_weight(jax.random.fold_in(keys[15], 71), 0),
        "value_weight": scatter_about(keys[4], (EMBED_SPAN, ATTN_CHANNELS), EMBED_SPAN ** -0.5, 0.125),
        "output_weight": scatter_about(keys[5], (ATTN_CHANNELS, EMBED_SPAN), ATTN_CHANNELS ** -0.5, 0.1875),
        "lengths": draw_lengths(jax.random.fold_in(keys[15], 71), 0),
        "request_adapter": draw_request_adapter(jax.random.fold_in(keys[15], 71), 0),
        "slot_adapter_ids": draw_slot_adapter_ids(jax.random.fold_in(keys[15], 71), 0),
        "plugin_shrink_maps": scatter_about(keys[9], (TOTAL_PLUGINS, EMBED_SPAN, 2 * LATENT_BREADTH), EMBED_SPAN ** -0.5, 0.125, ((0, 8),)),
        "plugin_grow_maps": scatter_about(keys[10], (TOTAL_PLUGINS, 2, LATENT_BREADTH, ATTN_CHANNELS), LATENT_BREADTH ** -0.5, 1.5, ((0, 8),)),
        "device_token_order": jax.vmap(lambda own: jax.random.permutation(own, TOK_DEV))(jax.random.split(keys[11], DEVICES)).reshape((DEVICES, TOK_DEV)).astype(jnp.int32),
        "second_norm_gain": jnp.clip(1.0 + 0.15 * jax.random.normal(keys[12], (EMBED_SPAN,), jnp.float32), 0.25, 1.75),
        "gate_weight": scatter_about(keys[13], (EMBED_SPAN, FF), EMBED_SPAN ** -0.5, 0.125, ((0, 32),)),
        "up_weight": scatter_about(keys[14], (EMBED_SPAN, FF), EMBED_SPAN ** -0.5, 0.125, ((0, 32),)),
    }


PLUGIN_STRENGTH = 2.0
EPSILON = 1e-05

def normalize(rows_in, gain_vec):
    floated = rows_in.astype(jnp.float32)
    scale = lax.rsqrt(lax.optimization_barrier(jnp.mean(floated * floated, axis=-1, keepdims=True)) + EPSILON)
    return (floated * scale * gain_vec.astype(jnp.float32)).astype(jnp.bfloat16)

def attend(query, key, value, request_len):
    queries = query.reshape(REQ_DEV, SLOTR, HEADS, HD).astype(jnp.float32)
    head_keys = key.reshape(REQ_DEV, SLOTR, HEADS, HD).astype(jnp.float32)
    head_values = value.reshape(REQ_DEV, SLOTR, HEADS, HD).astype(jnp.float32)
    scores = jnp.einsum('rqhd,rkhd->rhqk', queries, head_keys) * HD ** (-0.5)
    places = jnp.arange(SLOTR)
    query_place = places[:, None]
    key_place = places[None, :]
    allowed = (key_place <= query_place) & ((query_place - key_place < WINDOW) | (key_place < SINKS))
    key_live = places[None, :] < request_len[:, None]
    visible_lookup_flags = allowed[None, None, :, :] & key_live[:, None, None, :]
    scores = jnp.where(visible_lookup_flags, scores, -1e+30)
    row_max = lax.optimization_barrier(jnp.max(scores, axis=-1, keepdims=True))
    expo = jnp.where(visible_lookup_flags, jnp.exp(scores - row_max), 0.0)
    softmax_w = (expo / lax.optimization_barrier(jnp.sum(expo, axis=-1, keepdims=True))).astype(jnp.bfloat16)
    attended = jnp.einsum('rhqk,rkhd->rqhd', softmax_w.astype(jnp.float32), head_values).astype(jnp.bfloat16)
    query_live = (places[None, :] < request_len[:, None])[:, :, None, None]
    attended = jnp.where(query_live, attended, jnp.zeros_like(attended))
    return attended.reshape(REQ_DEV * SLOTR, HEADS * HD)

def reference(tokens, first_norm_gain, query_weight, key_weight, value_weight, output_weight, lengths, request_adapter, slot_adapter_ids, plugin_shrink_maps, plugin_grow_maps, device_token_order, second_norm_gain, gate_weight, up_weight):
    slot_of = jnp.zeros((TOTAL_PLUGINS,), jnp.int32).at[slot_adapter_ids].set(jnp.arange(TOTAL_PLUGINS, dtype=jnp.int32))
    slot_ids = slot_of[request_adapter].reshape(DEVICES, REQ_DEV)
    tok_dev = REQ_DEV * SLOTR
    hw_size = HEADS * HD

    def one_device(packed):
        rows_in, request_len, slots_per_device = packed
        normed = normalize(rows_in, first_norm_gain)
        down_matrices = plugin_shrink_maps[slots_per_device].astype(jnp.float32)
        growth_coefficients = plugin_grow_maps[slots_per_device].astype(jnp.float32)
        request_rows = normed.reshape(REQ_DEV, SLOTR, EMBED_SPAN).astype(jnp.float32)
        thin_latent_image = jnp.einsum('rsd,rdk->rsk', request_rows, down_matrices).astype(jnp.bfloat16).astype(jnp.float32)
        queries_lowrank_delta = (jnp.einsum('lce,lef->lcf', thin_latent_image[..., :LATENT_BREADTH], growth_coefficients[:, 0]) * PLUGIN_STRENGTH).astype(jnp.bfloat16)
        values_lowrank_delta = (jnp.einsum('lce,lef->lcf', thin_latent_image[..., LATENT_BREADTH:], growth_coefficients[:, 1]) * PLUGIN_STRENGTH).astype(jnp.bfloat16)
        query = (jnp.dot(normed, query_weight, preferred_element_type=jnp.float32) + queries_lowrank_delta.reshape(tok_dev, hw_size).astype(jnp.float32)).astype(jnp.bfloat16)
        key = jnp.dot(normed, key_weight, preferred_element_type=jnp.float32).astype(jnp.bfloat16)
        value = (jnp.dot(normed, value_weight, preferred_element_type=jnp.float32) + values_lowrank_delta.reshape(tok_dev, hw_size).astype(jnp.float32)).astype(jnp.bfloat16)
        attended = attend(query, key, value, request_len)
        mixed = rows_in.astype(jnp.float32) + jnp.dot(attended, output_weight, preferred_element_type=jnp.float32)
        return mixed.astype(jnp.bfloat16)
    residual = lax.map(one_device, (tokens.reshape(DEVICES, tok_dev, EMBED_SPAN), lengths.reshape(DEVICES, REQ_DEV), slot_ids))
    shuffled = jnp.take_along_axis(residual, device_token_order[:, :, None], axis=1)
    block_rows = tok_dev // DEVICES
    regrouped = shuffled.reshape(DEVICES, DEVICES, block_rows, EMBED_SPAN).transpose(1, 0, 2, 3)
    regrouped = regrouped.reshape(DEVICES, tok_dev, EMBED_SPAN)

    def gated(rows_in):
        mlp_input = normalize(rows_in, second_norm_gain)
        gate = jnp.dot(mlp_input, gate_weight, preferred_element_type=jnp.float32)
        upper = jnp.dot(mlp_input, up_weight, preferred_element_type=jnp.float32)
        return (jax.nn.silu(gate) * upper).astype(jnp.bfloat16)
    hidden = lax.map(gated, regrouped)
    return (residual.reshape(DEVICES * tok_dev, EMBED_SPAN), hidden.reshape(DEVICES * tok_dev, FF))
```

```python
import jax
import jax.numpy as jnp
from jax import lax
from jax.experimental import pallas as pl
from jax.experimental.pallas import tpu as pltpu
from jax.sharding import PartitionSpec as P

EMBED_SPAN = 1792
HEADS = 8
HD = 112
LATENT_BREADTH = 16
REQ_DEV = 8
SLOTR = 64
WINDOW = 32
SINKS = 4


PLUGIN_STRENGTH = 2.0
EPSILON = 1e-05


def normalize(rows_in, gain_vec):
    floated = rows_in.astype(jnp.float32)
    scale = lax.rsqrt(jnp.mean(floated * floated, axis=-1, keepdims=True) + EPSILON)
    return (floated * scale * gain_vec).astype(jnp.bfloat16)


def attend(query, key, value, request_len):
    queries = query.reshape(REQ_DEV, SLOTR, HEADS, HD)
    head_keys = key.reshape(REQ_DEV, SLOTR, HEADS, HD)
    head_values = value.reshape(REQ_DEV, SLOTR, HEADS, HD)
    scores = jnp.einsum(
        "rqhd,rkhd->rhqk", queries, head_keys, preferred_element_type=jnp.float32
    ) * HD ** (-0.5)
    places = jnp.arange(SLOTR)
    query_place = places[:, None]
    key_place = places[None, :]
    allowed = (key_place <= query_place) & (
        (query_place - key_place < WINDOW) | (key_place < SINKS)
    )
    key_live = places[None, :] < request_len[:, None]
    visible_lookup_flags = allowed[None, None, :, :] & key_live[:, None, None, :]
    scores = jnp.where(visible_lookup_flags, scores, -1e30)
    row_max = jnp.max(scores, axis=-1, keepdims=True)
    expo = jnp.where(visible_lookup_flags, jnp.exp(scores - row_max), 0.0)
    softmax_w = (expo / jnp.sum(expo, axis=-1, keepdims=True)).astype(jnp.bfloat16)
    attended = jnp.einsum(
        "rhqk,rkhd->rqhd", softmax_w, head_values, preferred_element_type=jnp.float32
    ).astype(jnp.bfloat16)
    query_live = (places[None, :] < request_len[:, None])[:, :, None, None]
    attended = jnp.where(query_live, attended, jnp.zeros_like(attended))
    return attended.reshape(REQ_DEV * SLOTR, HEADS * HD)


CORES = 2


def gated_kernel(own_ref, sib_ref, go_ref, gs_ref, uo_ref, us_ref, o_ref):
    own = own_ref[...]
    sib = sib_ref[...]
    gate = jnp.dot(own, go_ref[...], preferred_element_type=jnp.float32)
    gate += jnp.dot(sib, gs_ref[...], preferred_element_type=jnp.float32)
    up = jnp.dot(own, uo_ref[...], preferred_element_type=jnp.float32)
    up += jnp.dot(sib, us_ref[...], preferred_element_type=jnp.float32)
    o_ref[...] = (gate * jax.nn.sigmoid(gate) * up).astype(o_ref.dtype)


def gated(own, sib, gate_own, gate_sib, up_own, up_sib):
    rows, depth = own.shape
    width = gate_own.shape[1]
    tile = 512
    act = pl.BlockSpec((rows, depth), lambda i: (0, 0))
    wgt = pl.BlockSpec((depth, tile), lambda i: (0, i))
    return pl.pallas_call(
        gated_kernel,
        out_shape=jax.ShapeDtypeStruct((rows, width), jnp.bfloat16),
        grid=(width // tile,),
        in_specs=[act, act, wgt, wgt, wgt, wgt],
        out_specs=pl.BlockSpec((rows, tile), lambda i: (0, i)),
        compiler_params=pltpu.CompilerParams(vmem_limit_bytes=40 << 20),
        name="gated_units",
    )(own, sib, gate_own, gate_sib, up_own, up_sib)


def local(
    tokens,
    first_norm_gain,
    query_weight,
    key_weight,
    value_weight,
    output_weight,
    lengths,
    request_adapter,
    slot_adapter_ids,
    plugin_shrink_maps,
    plugin_grow_maps,
    device_token_order,
    second_norm_gain,
    gate_weight,
    up_weight,
):
    owner_count = lax.axis_size("mp")
    resident_slots = plugin_shrink_maps.shape[0]
    tok_dev = tokens.shape[0]
    hw_size = query_weight.shape[1]
    every = ("x", "core", "mp")
    swap = [(0, 1), (1, 0)]
    core = lax.axis_index("core")

    gate_own = lax.all_gather(gate_weight, ("x", "mp"), axis=0, tiled=True)
    up_own = lax.all_gather(up_weight, ("x", "mp"), axis=0, tiled=True)
    gate_sib = lax.ppermute(gate_own, "core", swap)
    up_sib = lax.ppermute(up_own, "core", swap)

    matches = (slot_adapter_ids[None, :] == request_adapter[:, None]).astype(jnp.int32)
    slot_ids = jnp.sum(
        matches * jnp.arange(slot_adapter_ids.shape[0], dtype=jnp.int32)[None, :], axis=1
    )
    owner_index = slot_ids // resident_slots
    within = slot_ids % resident_slots
    routing = (jnp.arange(owner_count)[:, None] == owner_index[None, :]).astype(jnp.bfloat16)
    slot_pick = (jnp.arange(resident_slots)[None, :] == within[:, None]).astype(jnp.bfloat16)
    chosen = jnp.dot(routing, slot_pick, preferred_element_type=jnp.float32).astype(jnp.bfloat16)
    chosen_adapter = lax.all_to_all(chosen, "mp", split_axis=0, concat_axis=0, tiled=True)
    maps = jnp.concatenate(
        [
            plugin_shrink_maps.transpose(0, 2, 1),
            plugin_grow_maps.reshape(resident_slots, 2 * LATENT_BREADTH, hw_size),
        ],
        axis=-1,
    )
    outgoing = jnp.einsum(
        "ge,ezc->gzc", chosen_adapter, maps, preferred_element_type=jnp.float32
    ).astype(jnp.bfloat16)
    incoming = lax.all_to_all(outgoing, "mp", split_axis=0, concat_axis=0, tiled=True)
    own_maps = jnp.einsum(
        "or,ozc->rzc", routing, incoming, preferred_element_type=jnp.float32
    ).astype(jnp.bfloat16)

    normed = normalize(tokens, first_norm_gain)
    request_rows = normed.reshape(REQ_DEV, SLOTR, EMBED_SPAN)
    codes = jnp.einsum(
        "rsd,rkd->rsk",
        request_rows,
        own_maps[..., :EMBED_SPAN],
        preferred_element_type=jnp.float32,
    ).astype(jnp.bfloat16)
    delta_q = (
        jnp.einsum(
            "rsk,rkh->rsh",
            codes[..., :LATENT_BREADTH],
            own_maps[:, :LATENT_BREADTH, EMBED_SPAN:],
            preferred_element_type=jnp.float32,
        )
        * PLUGIN_STRENGTH
    ).astype(jnp.bfloat16)
    delta_v = (
        jnp.einsum(
            "rsk,rkh->rsh",
            codes[..., LATENT_BREADTH:],
            own_maps[:, LATENT_BREADTH:, EMBED_SPAN:],
            preferred_element_type=jnp.float32,
        )
        * PLUGIN_STRENGTH
    ).astype(jnp.bfloat16)
    query = (
        jnp.dot(normed, query_weight, preferred_element_type=jnp.float32)
        + delta_q.reshape(tok_dev, hw_size).astype(jnp.float32)
    ).astype(jnp.bfloat16)
    key = jnp.dot(normed, key_weight, preferred_element_type=jnp.float32).astype(jnp.bfloat16)
    value = (
        jnp.dot(normed, value_weight, preferred_element_type=jnp.float32)
        + delta_v.reshape(tok_dev, hw_size).astype(jnp.float32)
    ).astype(jnp.bfloat16)
    attended = attend(query, key, value, lengths)
    residual = (
        tokens.astype(jnp.float32)
        + jnp.dot(attended, output_weight, preferred_element_type=jnp.float32)
    ).astype(jnp.bfloat16)
    order = (device_token_order[0][:, None] == jnp.arange(tok_dev)[None, :]).astype(jnp.bfloat16)
    shuffled = jnp.dot(order, residual, preferred_element_type=jnp.float32).astype(jnp.bfloat16)
    regrouped = lax.all_to_all(shuffled, every, split_axis=0, concat_axis=0, tiled=True)
    mlp_input = normalize(regrouped, second_norm_gain)
    by_core = mlp_input.reshape(tok_dev, lax.axis_size("x"), CORES, -1)
    even = by_core[:, :, 0].reshape(tok_dev, -1)
    odd = by_core[:, :, 1].reshape(tok_dev, -1)
    own = jnp.where(core == 0, even, odd)
    sib = jnp.where(core == 0, odd, even)
    hidden = gated(own, sib, gate_own, gate_sib, up_own, up_sib)
    return (residual, hidden)


def solution(mesh):
    dp, mp = mesh.devices.shape
    fine = jax.sharding.Mesh(mesh.devices.reshape(dp // CORES, CORES, mp), ("x", "core", "mp"))
    rows = ("x", "core", "mp")
    return jax.shard_map(
        local,
        mesh=fine,
        in_specs=(
            P(rows, None),
            P(),
            P(),
            P(),
            P(),
            P(),
            P(rows),
            P(rows),
            P(),
            P("mp", None, None),
            P("mp", None, None, None),
            P(rows, None),
            P(),
            P(rows, None),
            P(rows, None),
        ),
        out_specs=(P(rows, None), P(rows, None)),
        check_vma=False,
    )
```

```python
import functools

import jax
import jax.numpy as jnp
from jax import lax
from jax.experimental import pallas as pl
from jax.experimental.pallas import tpu as pltpu
from jax.sharding import PartitionSpec as P

EMBED_SPAN = 1792
HEADS = 8
HD = 112
LATENT_BREADTH = 16
REQ_DEV = 8
SLOTR = 64
WINDOW = 32
SINKS = 4


PLUGIN_STRENGTH = 2.0
EPSILON = 1e-05


def normalize(rows_in, gain_vec):
    floated = rows_in.astype(jnp.float32)
    scale = lax.rsqrt(jnp.mean(floated * floated, axis=-1, keepdims=True) + EPSILON)
    return (floated * scale * gain_vec).astype(jnp.bfloat16)


def attend(query, key, value, request_len):
    queries = query.reshape(REQ_DEV, SLOTR, HEADS, HD)
    head_keys = key.reshape(REQ_DEV, SLOTR, HEADS, HD)
    head_values = value.reshape(REQ_DEV, SLOTR, HEADS, HD)
    scores = jnp.einsum(
        "rqhd,rkhd->rhqk", queries, head_keys, preferred_element_type=jnp.float32
    ) * HD ** (-0.5)
    places = jnp.arange(SLOTR)
    query_place = places[:, None]
    key_place = places[None, :]
    allowed = (key_place <= query_place) & (
        (query_place - key_place < WINDOW) | (key_place < SINKS)
    )
    key_live = places[None, :] < request_len[:, None]
    visible_lookup_flags = allowed[None, None, :, :] & key_live[:, None, None, :]
    scores = jnp.where(visible_lookup_flags, scores, -1e30)
    row_max = jnp.max(scores, axis=-1, keepdims=True)
    expo = jnp.where(visible_lookup_flags, jnp.exp(scores - row_max), 0.0)
    softmax_w = (expo / jnp.sum(expo, axis=-1, keepdims=True)).astype(jnp.bfloat16)
    attended = jnp.einsum(
        "rhqk,rkhd->rqhd", softmax_w, head_values, preferred_element_type=jnp.float32
    ).astype(jnp.bfloat16)
    query_live = (places[None, :] < request_len[:, None])[:, :, None, None]
    attended = jnp.where(query_live, attended, jnp.zeros_like(attended))
    return attended.reshape(REQ_DEV * SLOTR, HEADS * HD)


CORES = 2


def gated_kernel(blocks, spots_ref, rows_ref, gain_ref, *refs):
    gate_refs = refs[: 2 * blocks]
    up_refs = refs[2 * blocks : 2 * blocks + 2]
    o_ref, act = refs[2 * blocks + 2 :]
    depth = act.shape[2]

    @pl.when(pl.program_id(0) == 0)
    def _():
        @pl.loop(0, rows_ref.shape[0], step=64)
        def _(r):
            part = pl.ds(pl.multiple_of(r, 64), 64)
            wide = rows_ref[part, :].astype(jnp.float32)
            scale = lax.rsqrt(jnp.mean(wide * wide, axis=-1, keepdims=True) + EPSILON)
            done = (wide * scale * gain_ref[...]).astype(jnp.bfloat16)
            for k in range(2 * blocks):
                act[k, part, :] = done[:, k * depth : (k + 1) * depth]

    gate = None
    up = None
    for k in range(2 * blocks):
        side, at = divmod(k, blocks)
        term = jnp.dot(
            act[spots_ref[k]], gate_refs[k][...], preferred_element_type=jnp.float32
        )
        gate = term if gate is None else gate + term
        term = jnp.dot(
            act[spots_ref[2 * blocks + k]],
            up_refs[side][at * depth : (at + 1) * depth, :],
            preferred_element_type=jnp.float32,
        )
        up = term if up is None else up + term
    o_ref[...] = (gate * jax.nn.sigmoid(gate) * up).astype(o_ref.dtype)


def gated(regrouped, gain, spots, gates, ups):
    rows, width_in = regrouped.shape
    width = gates[0].shape[1]
    blocks = len(gates) // 2
    depth = gates[0].shape[0]
    tile = 512
    whole = lambda i, spots: (0, 0)
    strip = lambda i, spots: (0, i)
    return pl.pallas_call(
        functools.partial(gated_kernel, blocks),
        out_shape=jax.ShapeDtypeStruct((rows, width), jnp.bfloat16),
        grid_spec=pltpu.PrefetchScalarGridSpec(
            num_scalar_prefetch=1,
            grid=(width // tile,),
            in_specs=[pl.BlockSpec((rows, width_in), whole), pl.BlockSpec((1, width_in), whole)]
            + [pl.BlockSpec((w.shape[0], tile), strip) for w in (*gates, *ups)],
            out_specs=pl.BlockSpec((rows, tile), strip),
            scratch_shapes=[pltpu.VMEM((2 * blocks, rows, depth), jnp.bfloat16)],
        ),
        compiler_params=pltpu.CompilerParams(vmem_limit_bytes=40 << 20),
        name="gated_units",
    )(spots, regrouped, gain[None, :], *gates, *ups)


def local(
    tokens,
    first_norm_gain,
    query_weight,
    key_weight,
    value_weight,
    output_weight,
    lengths,
    request_adapter,
    slot_adapter_ids,
    plugin_shrink_maps,
    plugin_grow_maps,
    device_token_order,
    second_norm_gain,
    gate_weight,
    up_weight,
):
    owner_count = lax.axis_size("mp")
    resident_slots = plugin_shrink_maps.shape[0]
    tok_dev = tokens.shape[0]
    hw_size = query_weight.shape[1]
    every = ("x", "core", "mp")
    swap = [(0, 1), (1, 0)]
    core = lax.axis_index("core")

    here = lax.axis_index("x")
    span = lax.axis_size("x")
    onward = [(i, (i + 1) % span) for i in range(span)]
    gate_own = lax.all_gather(gate_weight, "mp", axis=0, tiled=True)
    up_own = lax.all_gather(up_weight, ("x", "mp"), axis=0, tiled=True)

    matches = (slot_adapter_ids[None, :] == request_adapter[:, None]).astype(jnp.int32)
    slot_ids = jnp.sum(
        matches * jnp.arange(slot_adapter_ids.shape[0], dtype=jnp.int32)[None, :], axis=1
    )
    owner_index = slot_ids // resident_slots
    within = slot_ids % resident_slots
    routing = (jnp.arange(owner_count)[:, None] == owner_index[None, :]).astype(jnp.bfloat16)
    slot_pick = (jnp.arange(resident_slots)[None, :] == within[:, None]).astype(jnp.bfloat16)
    chosen = jnp.dot(routing, slot_pick, preferred_element_type=jnp.float32).astype(jnp.bfloat16)
    chosen_adapter = lax.all_to_all(chosen, "mp", split_axis=0, concat_axis=0, tiled=True)
    maps = jnp.concatenate(
        [
            plugin_shrink_maps.transpose(0, 2, 1),
            plugin_grow_maps.reshape(resident_slots, 2 * LATENT_BREADTH, hw_size),
        ],
        axis=-1,
    )
    outgoing = jnp.einsum(
        "ge,ezc->gzc", chosen_adapter, maps, preferred_element_type=jnp.float32
    ).astype(jnp.bfloat16)
    incoming = lax.all_to_all(outgoing, "mp", split_axis=0, concat_axis=0, tiled=True)
    own_maps = jnp.einsum(
        "or,ozc->rzc", routing, incoming, preferred_element_type=jnp.float32
    ).astype(jnp.bfloat16)

    normed = normalize(tokens, first_norm_gain)
    request_rows = normed.reshape(REQ_DEV, SLOTR, EMBED_SPAN)
    codes = jnp.einsum(
        "rsd,rkd->rsk",
        request_rows,
        own_maps[..., :EMBED_SPAN],
        preferred_element_type=jnp.float32,
    ).astype(jnp.bfloat16)
    delta_q = (
        jnp.einsum(
            "rsk,rkh->rsh",
            codes[..., :LATENT_BREADTH],
            own_maps[:, :LATENT_BREADTH, EMBED_SPAN:],
            preferred_element_type=jnp.float32,
        )
        * PLUGIN_STRENGTH
    ).astype(jnp.bfloat16)
    delta_v = (
        jnp.einsum(
            "rsk,rkh->rsh",
            codes[..., LATENT_BREADTH:],
            own_maps[:, LATENT_BREADTH:, EMBED_SPAN:],
            preferred_element_type=jnp.float32,
        )
        * PLUGIN_STRENGTH
    ).astype(jnp.bfloat16)
    query = (
        jnp.dot(normed, query_weight, preferred_element_type=jnp.float32)
        + delta_q.reshape(tok_dev, hw_size).astype(jnp.float32)
    ).astype(jnp.bfloat16)
    key = jnp.dot(normed, key_weight, preferred_element_type=jnp.float32).astype(jnp.bfloat16)
    value = (
        jnp.dot(normed, value_weight, preferred_element_type=jnp.float32)
        + delta_v.reshape(tok_dev, hw_size).astype(jnp.float32)
    ).astype(jnp.bfloat16)
    gate_own, key = lax.optimization_barrier((gate_own, key))
    gate_parts = [gate_own]
    for _ in range(span - 1):
        gate_parts.append(lax.ppermute(gate_parts[-1], "x", onward))
    attended = attend(query, key, value, lengths)
    residual = (
        tokens.astype(jnp.float32)
        + jnp.dot(attended, output_weight, preferred_element_type=jnp.float32)
    ).astype(jnp.bfloat16)
    places = device_token_order.reshape(-1, tok_dev // lax.axis_size(every))
    half = places.shape[1] // 2
    halves = []
    for picked in (places[:, :half], places[:, half:]):
        chosen_rows = picked.reshape(-1, 1) == jnp.arange(tok_dev)[None, :]
        part = jnp.dot(
            chosen_rows.astype(jnp.bfloat16), residual, preferred_element_type=jnp.float32
        ).astype(jnp.bfloat16)
        part = part.reshape(places.shape[0], half, EMBED_SPAN)
        halves.append(lax.all_to_all(part, every, split_axis=0, concat_axis=0, tiled=True))
    gate_parts, up_own, halves[0] = lax.optimization_barrier((gate_parts, up_own, halves[0]))
    regrouped = jnp.concatenate(halves, axis=1).reshape(tok_dev, EMBED_SPAN)
    gate_parts = gate_parts + [lax.ppermute(part, "core", swap) for part in gate_parts]
    up_sib = lax.ppermute(up_own, "core", swap)
    ahead = jnp.arange(span)
    walk = (here - ahead + span) % span
    spots = jnp.concatenate(
        [walk * CORES + core, walk * CORES + 1 - core, ahead * CORES + core, ahead * CORES + 1 - core]
    ).astype(jnp.int32)
    hidden = gated(regrouped, second_norm_gain, spots, gate_parts, [up_own, up_sib])
    return (residual, hidden)


def solution(mesh):
    dp, mp = mesh.devices.shape
    fine = jax.sharding.Mesh(mesh.devices.reshape(dp // CORES, CORES, mp), ("x", "core", "mp"))
    rows = ("x", "core", "mp")
    return jax.shard_map(
        local,
        mesh=fine,
        in_specs=(
            P(rows, None),
            P(),
            P(),
            P(),
            P(),
            P(),
            P(rows),
            P(rows),
            P(),
            P("mp", None, None),
            P("mp", None, None, None),
            P(rows, None),
            P(),
            P(rows, None),
            P(rows, None),
        ),
        out_specs=(P(rows, None), P(rows, None)),
        check_vma=False,
    )
```

```python
import jax
import jax.numpy as jnp
from jax import lax
from jax.experimental import pallas as pl
from jax.experimental.pallas import tpu as pltpu
from jax.sharding import PartitionSpec as P

EMBED_SPAN = 1792
HEADS = 8
HD = 112
LATENT_BREADTH = 16
REQ_DEV = 8
SLOTR = 64
WINDOW = 32
SINKS = 4


PLUGIN_STRENGTH = 2.0
EPSILON = 1e-05


def normalize(rows_in, gain_vec):
    floated = rows_in.astype(jnp.float32)
    scale = lax.rsqrt(jnp.mean(floated * floated, axis=-1, keepdims=True) + EPSILON)
    return (floated * scale * gain_vec).astype(jnp.bfloat16)


def attend(query, key, value, request_len):
    queries = query.reshape(REQ_DEV, SLOTR, HEADS, HD)
    head_keys = key.reshape(REQ_DEV, SLOTR, HEADS, HD)
    head_values = value.reshape(REQ_DEV, SLOTR, HEADS, HD)
    scores = jnp.einsum(
        "rqhd,rkhd->rhqk", queries, head_keys, preferred_element_type=jnp.float32
    ) * HD ** (-0.5)
    places = jnp.arange(SLOTR)
    query_place = places[:, None]
    key_place = places[None, :]
    allowed = (key_place <= query_place) & (
        (query_place - key_place < WINDOW) | (key_place < SINKS)
    )
    key_live = places[None, :] < request_len[:, None]
    visible_lookup_flags = allowed[None, None, :, :] & key_live[:, None, None, :]
    scores = jnp.where(visible_lookup_flags, scores, -1e30)
    row_max = jnp.max(scores, axis=-1, keepdims=True)
    expo = jnp.where(visible_lookup_flags, jnp.exp(scores - row_max), 0.0)
    softmax_w = (expo / jnp.sum(expo, axis=-1, keepdims=True)).astype(jnp.bfloat16)
    attended = jnp.einsum(
        "rhqk,rkhd->rqhd", softmax_w, head_values, preferred_element_type=jnp.float32
    ).astype(jnp.bfloat16)
    query_live = (places[None, :] < request_len[:, None])[:, :, None, None]
    attended = jnp.where(query_live, attended, jnp.zeros_like(attended))
    return attended.reshape(REQ_DEV * SLOTR, HEADS * HD)


CORES = 2


def gate_kernel(rows_ref, gain_ref, w_ref, act_ref, o_ref):
    @pl.when(pl.program_id(0) == 0)
    def _():
        @pl.loop(0, rows_ref.shape[0], step=64)
        def _(r):
            part = pl.ds(pl.multiple_of(r, 64), 64)
            wide = rows_ref[part, :].astype(jnp.float32)
            scale = lax.rsqrt(jnp.mean(wide * wide, axis=-1, keepdims=True) + EPSILON)
            act_ref[part, :] = (wide * scale * gain_ref[...]).astype(jnp.bfloat16)

    gate = jnp.dot(act_ref[...], w_ref[...], preferred_element_type=jnp.float32)
    o_ref[...] = gate * jax.nn.sigmoid(gate)


def gate_units(regrouped, gain, weight):
    rows, depth = regrouped.shape
    width = weight.shape[1]
    tile = 512
    whole = lambda i: (0, 0)
    strip = lambda i: (0, i)
    return pl.pallas_call(
        gate_kernel,
        out_shape=(
            jax.ShapeDtypeStruct((rows, depth), jnp.bfloat16),
            jax.ShapeDtypeStruct((rows, width), jnp.float32),
        ),
        grid=(width // tile,),
        in_specs=[
            pl.BlockSpec((rows, depth), whole),
            pl.BlockSpec((1, depth), whole),
            pl.BlockSpec((depth, tile), strip),
        ],
        out_specs=(pl.BlockSpec((rows, depth), whole), pl.BlockSpec((rows, tile), strip)),
        compiler_params=pltpu.CompilerParams(vmem_limit_bytes=32 << 20),
        name="gate_units",
    )(regrouped, gain[None, :], weight)


def up_kernel(act_ref, silu_ref, w_ref, o_ref):
    up = jnp.dot(act_ref[...], w_ref[...], preferred_element_type=jnp.float32)
    o_ref[...] = (silu_ref[...] * up).astype(o_ref.dtype)


def up_units(act, silu, weight):
    rows, depth = act.shape
    width = weight.shape[1]
    tile = 512
    strip = lambda i: (0, i)
    return pl.pallas_call(
        up_kernel,
        out_shape=jax.ShapeDtypeStruct((rows, width), jnp.bfloat16),
        grid=(width // tile,),
        in_specs=[
            pl.BlockSpec((rows, depth), lambda i: (0, 0)),
            pl.BlockSpec((rows, tile), strip),
            pl.BlockSpec((depth, tile), strip),
        ],
        out_specs=pl.BlockSpec((rows, tile), strip),
        compiler_params=pltpu.CompilerParams(vmem_limit_bytes=48 << 20),
        name="up_units",
    )(act, silu, weight)


def local(
    tokens,
    first_norm_gain,
    query_weight,
    key_weight,
    value_weight,
    output_weight,
    lengths,
    request_adapter,
    slot_adapter_ids,
    plugin_shrink_maps,
    plugin_grow_maps,
    device_token_order,
    second_norm_gain,
    gate_weight,
    up_weight,
):
    owner_count = lax.axis_size("mp")
    resident_slots = plugin_shrink_maps.shape[0]
    tok_dev = tokens.shape[0]
    hw_size = query_weight.shape[1]
    every = ("x", "core", "mp")

    gate_full = lax.all_gather(gate_weight, every, axis=0, tiled=True)
    up_full = lax.all_gather(up_weight, every, axis=0, tiled=True)

    matches = (slot_adapter_ids[None, :] == request_adapter[:, None]).astype(jnp.int32)
    slot_ids = jnp.sum(
        matches * jnp.arange(slot_adapter_ids.shape[0], dtype=jnp.int32)[None, :], axis=1
    )
    owner_index = slot_ids // resident_slots
    within = slot_ids % resident_slots
    routing = (jnp.arange(owner_count)[:, None] == owner_index[None, :]).astype(jnp.bfloat16)
    slot_pick = (jnp.arange(resident_slots)[None, :] == within[:, None]).astype(jnp.bfloat16)
    chosen = jnp.dot(routing, slot_pick, preferred_element_type=jnp.float32).astype(jnp.bfloat16)
    chosen_adapter = lax.all_to_all(chosen, "mp", split_axis=0, concat_axis=0, tiled=True)
    maps = jnp.concatenate(
        [
            plugin_shrink_maps.transpose(0, 2, 1),
            plugin_grow_maps.reshape(resident_slots, 2 * LATENT_BREADTH, hw_size),
        ],
        axis=-1,
    )
    outgoing = jnp.einsum(
        "ge,ezc->gzc", chosen_adapter, maps, preferred_element_type=jnp.float32
    ).astype(jnp.bfloat16)
    incoming = lax.all_to_all(outgoing, "mp", split_axis=0, concat_axis=0, tiled=True)
    own_maps = jnp.einsum(
        "or,ozc->rzc", routing, incoming, preferred_element_type=jnp.float32
    ).astype(jnp.bfloat16)

    normed = normalize(tokens, first_norm_gain)
    request_rows = normed.reshape(REQ_DEV, SLOTR, EMBED_SPAN)
    codes = jnp.einsum(
        "rsd,rkd->rsk",
        request_rows,
        own_maps[..., :EMBED_SPAN],
        preferred_element_type=jnp.float32,
    ).astype(jnp.bfloat16)
    delta_q = (
        jnp.einsum(
            "rsk,rkh->rsh",
            codes[..., :LATENT_BREADTH],
            own_maps[:, :LATENT_BREADTH, EMBED_SPAN:],
            preferred_element_type=jnp.float32,
        )
        * PLUGIN_STRENGTH
    ).astype(jnp.bfloat16)
    delta_v = (
        jnp.einsum(
            "rsk,rkh->rsh",
            codes[..., LATENT_BREADTH:],
            own_maps[:, LATENT_BREADTH:, EMBED_SPAN:],
            preferred_element_type=jnp.float32,
        )
        * PLUGIN_STRENGTH
    ).astype(jnp.bfloat16)
    query = (
        jnp.dot(normed, query_weight, preferred_element_type=jnp.float32)
        + delta_q.reshape(tok_dev, hw_size).astype(jnp.float32)
    ).astype(jnp.bfloat16)
    key = jnp.dot(normed, key_weight, preferred_element_type=jnp.float32).astype(jnp.bfloat16)
    value = (
        jnp.dot(normed, value_weight, preferred_element_type=jnp.float32)
        + delta_v.reshape(tok_dev, hw_size).astype(jnp.float32)
    ).astype(jnp.bfloat16)
    attended = attend(query, key, value, lengths)
    residual = (
        tokens.astype(jnp.float32)
        + jnp.dot(attended, output_weight, preferred_element_type=jnp.float32)
    ).astype(jnp.bfloat16)
    order = device_token_order.reshape(-1, 1) == jnp.arange(tok_dev)[None, :]
    shuffled = jnp.dot(
        order.astype(jnp.bfloat16), residual, preferred_element_type=jnp.float32
    ).astype(jnp.bfloat16)
    regrouped = lax.all_to_all(shuffled, every, split_axis=0, concat_axis=0, tiled=True)
    act, silu = gate_units(regrouped, second_norm_gain, gate_full)
    hidden = up_units(act, silu, up_full)
    return (residual, hidden)


def solution(mesh):
    dp, mp = mesh.devices.shape
    fine = jax.sharding.Mesh(mesh.devices.reshape(dp // CORES, CORES, mp), ("x", "core", "mp"))
    rows = ("x", "core", "mp")
    return jax.shard_map(
        local,
        mesh=fine,
        in_specs=(
            P(rows, None),
            P(),
            P(),
            P(),
            P(),
            P(),
            P(rows),
            P(rows),
            P(),
            P("mp", None, None),
            P("mp", None, None, None),
            P(rows, None),
            P(),
            P(rows, None),
            P(rows, None),
        ),
        out_specs=(P(rows, None), P(rows, None)),
        check_vma=False,
    )
```

```python
import jax
import jax.numpy as jnp
from jax import lax
from jax.experimental import pallas as pl
from jax.experimental.pallas import tpu as pltpu
from jax.sharding import PartitionSpec as P

EMBED_SPAN = 1792
HEADS = 8
HD = 112
LATENT_BREADTH = 16
REQ_DEV = 8
SLOTR = 64
WINDOW = 32
SINKS = 4


PLUGIN_STRENGTH = 2.0
EPSILON = 1e-05


def normalize(rows_in, gain_vec):
    floated = rows_in.astype(jnp.float32)
    scale = lax.rsqrt(jnp.mean(floated * floated, axis=-1, keepdims=True) + EPSILON)
    return (floated * scale * gain_vec).astype(jnp.bfloat16)


def attend(query, key, value, request_len):
    queries = query.reshape(REQ_DEV, SLOTR, HEADS, HD)
    head_keys = key.reshape(REQ_DEV, SLOTR, HEADS, HD)
    head_values = value.reshape(REQ_DEV, SLOTR, HEADS, HD)
    scores = jnp.einsum(
        "rqhd,rkhd->rhqk", queries, head_keys, preferred_element_type=jnp.float32
    ) * HD ** (-0.5)
    places = jnp.arange(SLOTR)
    query_place = places[:, None]
    key_place = places[None, :]
    allowed = (key_place <= query_place) & (
        (query_place - key_place < WINDOW) | (key_place < SINKS)
    )
    key_live = places[None, :] < request_len[:, None]
    visible_lookup_flags = allowed[None, None, :, :] & key_live[:, None, None, :]
    scores = jnp.where(visible_lookup_flags, scores, -1e30)
    row_max = jnp.max(scores, axis=-1, keepdims=True)
    expo = jnp.where(visible_lookup_flags, jnp.exp(scores - row_max), 0.0)
    softmax_w = (expo / jnp.sum(expo, axis=-1, keepdims=True)).astype(jnp.bfloat16)
    attended = jnp.einsum(
        "rhqk,rkhd->rqhd", softmax_w, head_values, preferred_element_type=jnp.float32
    ).astype(jnp.bfloat16)
    query_live = (places[None, :] < request_len[:, None])[:, :, None, None]
    attended = jnp.where(query_live, attended, jnp.zeros_like(attended))
    return attended.reshape(REQ_DEV * SLOTR, HEADS * HD)


CORES = 2


def gate_kernel(rows_ref, gain_ref, w_ref, act_ref, o_ref):
    @pl.when(pl.program_id(0) == 0)
    def _():
        @pl.loop(0, rows_ref.shape[0], step=64)
        def _(r):
            part = pl.ds(pl.multiple_of(r, 64), 64)
            wide = rows_ref[part, :].astype(jnp.float32)
            scale = lax.rsqrt(jnp.mean(wide * wide, axis=-1, keepdims=True) + EPSILON)
            act_ref[part, :] = (wide * scale * gain_ref[...]).astype(jnp.bfloat16)

    gate = jnp.dot(act_ref[...], w_ref[...], preferred_element_type=jnp.float32)
    o_ref[...] = gate * jax.nn.sigmoid(gate)


def gate_units(regrouped, gain, weight):
    rows, depth = regrouped.shape
    width = weight.shape[1]
    tile = 512
    whole = lambda i: (0, 0)
    strip = lambda i: (0, i)
    return pl.pallas_call(
        gate_kernel,
        out_shape=(
            jax.ShapeDtypeStruct((rows, depth), jnp.bfloat16),
            jax.ShapeDtypeStruct((rows, width), jnp.float32),
        ),
        grid=(width // tile,),
        in_specs=[
            pl.BlockSpec((rows, depth), whole),
            pl.BlockSpec((1, depth), whole),
            pl.BlockSpec((depth, tile), strip),
        ],
        out_specs=(pl.BlockSpec((rows, depth), whole), pl.BlockSpec((rows, tile), strip)),
        compiler_params=pltpu.CompilerParams(vmem_limit_bytes=32 << 20),
        name="gate_units",
    )(regrouped, gain[None, :], weight)


def up_kernel(act_ref, silu_ref, w_ref, *refs):
    up = jnp.dot(act_ref[...], w_ref[...], preferred_element_type=jnp.float32)
    refs[-1][...] = (silu_ref[...] * up).astype(refs[-1].dtype)


def up_units(act, silu, weight, first, earlier=None):
    rows, depth = act.shape
    tile = 512
    strip = lambda i: (0, i + first // tile)
    given = [] if earlier is None else [earlier]
    return pl.pallas_call(
        up_kernel,
        out_shape=jax.ShapeDtypeStruct(silu.shape, jnp.bfloat16),
        grid=(weight.shape[1] // tile,),
        in_specs=[
            pl.BlockSpec((rows, depth), lambda i: (0, 0)),
            pl.BlockSpec((rows, tile), strip),
            pl.BlockSpec((depth, tile), lambda i: (0, i)),
        ]
        + [pl.BlockSpec(memory_space=pl.ANY) for _ in given],
        out_specs=pl.BlockSpec((rows, tile), strip),
        input_output_aliases={3: 0} if given else {},
        compiler_params=pltpu.CompilerParams(vmem_limit_bytes=48 << 20),
        name="up_units",
    )(act, silu, weight, *given)


def local(
    tokens,
    first_norm_gain,
    query_weight,
    key_weight,
    value_weight,
    output_weight,
    lengths,
    request_adapter,
    slot_adapter_ids,
    plugin_shrink_maps,
    plugin_grow_maps,
    device_token_order,
    second_norm_gain,
    gate_weight,
    up_weight,
):
    owner_count = lax.axis_size("mp")
    resident_slots = plugin_shrink_maps.shape[0]
    tok_dev = tokens.shape[0]
    hw_size = query_weight.shape[1]
    every = ("x", "core", "mp")

    gate_full = lax.all_gather(gate_weight, every, axis=0, tiled=True)
    early = up_weight.shape[1] * 5 // 7
    up_early = lax.all_gather(up_weight[:, :early], every, axis=0, tiled=True)
    up_late = lax.all_gather(up_weight[:, early:], every, axis=0, tiled=True)

    matches = (slot_adapter_ids[None, :] == request_adapter[:, None]).astype(jnp.int32)
    slot_ids = jnp.sum(
        matches * jnp.arange(slot_adapter_ids.shape[0], dtype=jnp.int32)[None, :], axis=1
    )
    owner_index = slot_ids // resident_slots
    within = slot_ids % resident_slots
    routing = (jnp.arange(owner_count)[:, None] == owner_index[None, :]).astype(jnp.bfloat16)
    slot_pick = (jnp.arange(resident_slots)[None, :] == within[:, None]).astype(jnp.bfloat16)
    chosen = jnp.dot(routing, slot_pick, preferred_element_type=jnp.float32).astype(jnp.bfloat16)
    chosen_adapter = lax.all_to_all(chosen, "mp", split_axis=0, concat_axis=0, tiled=True)
    maps = jnp.concatenate(
        [
            plugin_shrink_maps.transpose(0, 2, 1),
            plugin_grow_maps.reshape(resident_slots, 2 * LATENT_BREADTH, hw_size),
        ],
        axis=-1,
    )
    outgoing = jnp.einsum(
        "ge,ezc->gzc", chosen_adapter, maps, preferred_element_type=jnp.float32
    ).astype(jnp.bfloat16)
    incoming = lax.all_to_all(outgoing, "mp", split_axis=0, concat_axis=0, tiled=True)
    own_maps = jnp.einsum(
        "or,ozc->rzc", routing, incoming, preferred_element_type=jnp.float32
    ).astype(jnp.bfloat16)

    normed = normalize(tokens, first_norm_gain)
    request_rows = normed.reshape(REQ_DEV, SLOTR, EMBED_SPAN)
    codes = jnp.einsum(
        "rsd,rkd->rsk",
        request_rows,
        own_maps[..., :EMBED_SPAN],
        preferred_element_type=jnp.float32,
    ).astype(jnp.bfloat16)
    delta_q = (
        jnp.einsum(
            "rsk,rkh->rsh",
            codes[..., :LATENT_BREADTH],
            own_maps[:, :LATENT_BREADTH, EMBED_SPAN:],
            preferred_element_type=jnp.float32,
        )
        * PLUGIN_STRENGTH
    ).astype(jnp.bfloat16)
    delta_v = (
        jnp.einsum(
            "rsk,rkh->rsh",
            codes[..., LATENT_BREADTH:],
            own_maps[:, LATENT_BREADTH:, EMBED_SPAN:],
            preferred_element_type=jnp.float32,
        )
        * PLUGIN_STRENGTH
    ).astype(jnp.bfloat16)
    query = (
        jnp.dot(normed, query_weight, preferred_element_type=jnp.float32)
        + delta_q.reshape(tok_dev, hw_size).astype(jnp.float32)
    ).astype(jnp.bfloat16)
    key = jnp.dot(normed, key_weight, preferred_element_type=jnp.float32).astype(jnp.bfloat16)
    value = (
        jnp.dot(normed, value_weight, preferred_element_type=jnp.float32)
        + delta_v.reshape(tok_dev, hw_size).astype(jnp.float32)
    ).astype(jnp.bfloat16)
    attended = attend(query, key, value, lengths)
    residual = (
        tokens.astype(jnp.float32)
        + jnp.dot(attended, output_weight, preferred_element_type=jnp.float32)
    ).astype(jnp.bfloat16)
    order = device_token_order.reshape(-1, 1) == jnp.arange(tok_dev)[None, :]
    shuffled = jnp.dot(
        order.astype(jnp.bfloat16), residual, preferred_element_type=jnp.float32
    ).astype(jnp.bfloat16)
    regrouped = lax.all_to_all(shuffled, every, split_axis=0, concat_axis=0, tiled=True)
    act, silu = gate_units(regrouped, second_norm_gain, gate_full)
    hidden = up_units(act, silu, up_early, 0)
    hidden = up_units(act, silu, up_late, early, hidden)
    return (residual, hidden)


def solution(mesh):
    dp, mp = mesh.devices.shape
    fine = jax.sharding.Mesh(mesh.devices.reshape(dp // CORES, CORES, mp), ("x", "core", "mp"))
    rows = ("x", "core", "mp")
    return jax.shard_map(
        local,
        mesh=fine,
        in_specs=(
            P(rows, None),
            P(),
            P(),
            P(),
            P(),
            P(),
            P(rows),
            P(rows),
            P(),
            P("mp", None, None),
            P("mp", None, None, None),
            P(rows, None),
            P(),
            P(rows, None),
            P(rows, None),
        ),
        out_specs=(P(rows, None), P(rows, None)),
        check_vma=False,
    )
```
